512 devices in a mesh: req: 128 (over z_lo, y, x), tp: 4 (over z_hi, core).
Axes of the slice: x: 4, y: 8, z: 8 (z_hi: 2, z_lo: 4; z = z_hi * 4 + z_lo), core: 2. Of those that a mesh axis runs over, the one named last changes fastest.
Arguments:
- tokens: bfloat16 [8192, 2048], P('req', 'tp'), may hold values from -6 to 6
- expert_in: bfloat16 [128, 2, 2048, 1408], P('req', None, None, 'tp'), may hold values from -0.125 to 0.125
- expert_down: bfloat16 [128, 1408, 2048], P('req', 'tp'), may hold values from -0.15625 to 0.15625
- routes: int32 [8192, 6], P('req'), may hold values from 0 to 127, all different within a row; in each aligned block of 64 rows (0 to 63, 64 to 127, ...) at most 4 rows name the same one
- route_weight: float32 [8192, 6], P('req'), may hold values from 0.1 to 1
Outputs:
- mixed_out: bfloat16 [8192, 2048], P('req', 'tp')
The draws below stay inside these ranges and needn't reach their ends.
Inputs may be any that keep to these rules, and one draw needn't show every extreme that they name: `routes`: each row names 6 different experts. In each aligned block of 64 rows (the rows of one index of req) no expert is named by more than 4 rows, a bound that some block reaches; every expert is named somewhere.
All inputs are finite; a program needn't handle non-finite values.
Results may differ from the reference program's by a relative error of at most 0.012.
Values may be sent and summed in bfloat16 or wider, within the bound.
A program may use at most 64 MiB of HBM per device.

```python
import math
import jax
import jax.numpy as jnp
import numpy as np
from jax import lax

D = 2048
FF = 1408
TOP = 6
TOK_DEV = 64
EXPERTS = 128
TOKENS = 8192
CAP = 4
N_REQ = 128
N_TP = 4


def level_of(own_key, extent, cuts, least, high):
    loudness, own = 1.0, jax.random.fold_in(own_key, 6)
    for dim, parts in cuts:
        heights = jnp.exp(jax.random.uniform(jax.random.fold_in(own, dim), (parts,), jnp.float32, least / len(cuts), high / len(cuts)))
        loudness = loudness * jnp.repeat(heights, extent[dim] // parts).reshape([-1 if axis == dim else 1 for axis in range(len(extent))])
    return loudness


def assign_block(key, own, number, rows, amount, top, reach, lean):
    order = jax.random.permutation(key, amount)
    crowded, common = shares(amount, rows * top, reach, lean, True), shares(amount, rows * top, reach, lean, False)
    places = jnp.arange(amount)

    def named(lengths, turn):
        used = int((lengths > 0).sum())
        fixed = max(1, used // 4)
        shifted = fixed + (places - fixed + turn * (used - fixed)) % max(1, amount - fixed)
        return jnp.zeros((amount,), jnp.int32).at[order[jnp.where(places < fixed, places, shifted)]].set(jnp.asarray(lengths, jnp.int32))

    lengths = jnp.where(number % 4 == 0, named(crowded, number // 4), named(common, number - number // 4 - 1))
    mixed = jax.random.permutation(jax.random.fold_in(own, 3), amount)
    giver, receiver = mixed[0:amount // 2 * 2:2], mixed[1:amount // 2 * 2:2]
    room = jnp.minimum(lengths[giver] - 1, reach - lengths[receiver]) // 2
    room = jnp.where((giver == order[0]) | (receiver == order[0]) | (lengths[receiver] == 0), 0, jnp.maximum(room, 0))
    shifted = jax.random.randint(jax.random.fold_in(own, 4), (amount // 2,), 0, 1 << 20) % (room + 1)
    lengths = lengths.at[giver].add(-shifted).at[receiver].add(shifted)
    labels = jnp.searchsorted(jnp.cumsum(lengths), jnp.arange(rows * top), side="right").astype(jnp.int32)
    listing = labels.reshape(top, rows).T
    listing = listing[jax.random.permutation(jax.random.fold_in(own, 1), rows)]
    turn = jax.random.randint(jax.random.fold_in(own, 2), (rows, 1), 0, top)
    return jnp.take_along_axis(listing, (jnp.arange(top)[None, :] + turn) % top, axis=1)


def shares(amount, total, limit, slope, full):
    loads = [(1 << 20) // math.isqrt(grade ** slope) + 1 for grade in range(1, amount + 1)]
    largest = limit if full else min(limit, max(-(-total // amount), total * loads[0] // sum(loads)))
    least = 1 if total - largest >= amount - 1 else 0
    given, rest = [largest] + [least] * (amount - 1), total - largest - least * (amount - 1)
    while rest > 0:
        movable = [i for i in range(1, amount) if given[i] < largest] or [i for i in range(1, amount) if given[i] < limit]
        pool, budget = sum([loads[i] for i in movable]), rest
        for i in movable:
            extra = min(limit - given[i], max(1, budget * loads[i] // pool), rest)
            given[i] = given[i] + extra
            rest = rest - extra
    return np.array(given)


def gaussian(stream_key, extent, width, most, shards=(), kind=jnp.bfloat16):
    level = level_of(stream_key, extent, shards, -0.22, 0.18) if shards else 1.0
    result = jax.random.normal(stream_key, extent, jnp.float32) * width * level
    return jnp.minimum(jnp.maximum(result, -most), most).astype(kind)


def setup_inputs(seed: int = 0) -> dict:
    key_list = jax.random.split(jax.random.key(seed), 6)
    tokens = gaussian(key_list[0], (TOKENS, D), 1.0, 6.0, ((0, 128), (1, 4)))
    expert_in = gaussian(key_list[1], (EXPERTS, 2, D, FF), D ** -0.5, 0.125, ((0, 128), (3, 4)))
    expert_down = gaussian(key_list[2], (EXPERTS, FF, D), FF ** -0.5, 0.15625, ((0, 128), (1, 4)))
    routes_keys = jax.random.split(jax.random.fold_in(key_list[3], 1), TOKENS // TOK_DEV)
    routes_turns = jax.random.permutation(jax.random.fold_in(key_list[3], 3), TOKENS // TOK_DEV)
    routes = jax.vmap(lambda own, number: assign_block(jax.random.fold_in(key_list[3], 2), own, number, TOK_DEV, EXPERTS, TOP, CAP, 2))(routes_keys, routes_turns).reshape((TOKENS, TOP))
    route_weight = jnp.clip(0.1 + 0.9 * jax.random.uniform(key_list[4], (TOKENS, TOP), jnp.float32) ** level_of(key_list[4], (TOKENS, TOP), ((0, 128),), -0.2, 0.2), 0.1, 1.0)
    return {"tokens": tokens, "expert_in": expert_in, "expert_down": expert_down, "routes": routes, "route_weight": route_weight}


def reference(tokens, expert_in, expert_down, routes, route_weight):
    blocks = routes.reshape(N_REQ, TOK_DEV * TOP)
    onehot = (blocks[:, :, None] == jnp.arange(EXPERTS, dtype=jnp.int32)[None, None, :]).astype(jnp.int32)
    earlier = jnp.cumsum(onehot, axis=1) - onehot
    slot_index = jnp.sum(earlier * onehot, axis=2).astype(jnp.int32)
    source = jnp.arange(N_REQ, dtype=jnp.int32)[:, None]
    buffer_row = (source * CAP + slot_index).reshape(TOKENS, TOP).astype(jnp.int32)
    token_id = jnp.broadcast_to(jnp.arange(TOKENS, dtype=jnp.int32)[:, None], (TOKENS, TOP))
    row_table = jnp.full((EXPERTS, N_REQ * CAP), TOKENS, dtype=jnp.int32).at[routes, buffer_row].set(token_id)
    padded = jnp.concatenate([tokens, jnp.zeros((1, D), tokens.dtype)], axis=0)
    split_width = FF // N_TP

    def one_expert(operands):
        table_row, weights_in, weights_down = operands
        row_block = padded[table_row]
        gate_sums = jnp.dot(row_block, weights_in[0], preferred_element_type=jnp.float32)
        up_sums = jnp.dot(row_block, weights_in[1], preferred_element_type=jnp.float32)
        hidden = (jax.nn.silu(gate_sums) * up_sums).astype(jnp.bfloat16)
        running = jnp.zeros((N_REQ * CAP, D), jnp.float32)
        for group in range(N_TP):
            partial_value = jnp.dot(hidden[:, group * split_width:(group + 1) * split_width],
                              weights_down[group * split_width:(group + 1) * split_width],
                              preferred_element_type=jnp.float32)
            partial_value = lax.optimization_barrier(partial_value.astype(jnp.bfloat16)).astype(jnp.float32)
            running = running + partial_value
        return running.astype(jnp.bfloat16)

    results = lax.map(one_expert, (row_table, expert_in, expert_down))
    picked = results[routes, buffer_row]
    mixed_out = jnp.sum(route_weight[:, :, None] * picked.astype(jnp.float32), axis=1)
    return mixed_out.astype(jnp.bfloat16)
```

```python
import jax
import jax.numpy as jnp
from jax import lax
from jax.experimental import pallas as pl
from jax.experimental.pallas import tpu as pltpu
from jax.sharding import PartitionSpec as P

MESH = pl.DeviceIdType.MESH
TOK, TOP, CAP = 64, 6, 4
PLANE, RUN, RING = 32, 4, 8
ROWS = PLANE * RUN * CAP
GRP, FFG = 512, 352
HALF = 2 * GRP
MBLK = 256


def kernel(tok, rt, wt, win_hbm, wdn_hbm, out,
           win, wdn, tok_all, meta, xsend, xrecv, xoth, psend, precv, pown, sbuf, back,
           cw_hi, cw_lo, rsend, rrecv,
           w_sem, tok_s, tok_r, meta_s, meta_r, x_s, x_r, o_s, o_r, p_s, p_r, b_s, b_r,
           q_s, q_r):
    req, tp = lax.axis_index("req"), lax.axis_index("tp")
    zlo, here = lax.div(req, PLANE), lax.rem(req, PLANE)
    zhi, core = lax.div(tp, 2), lax.rem(tp, 2)
    z = zhi * RUN + zlo

    def in_plane(d):
        other = lax.rem(here + d, PLANE)
        return other, (zlo * PLANE + other, tp)

    def in_ring(d):
        other = lax.rem(z + d, RING)
        return other, (lax.rem(other, RUN) * PLANE + here, lax.div(other, RUN) * 2 + core)

    mate = (req, zhi * 2 + 1 - core)

    def remote(src, dst, s, r, to):
        return pltpu.make_async_remote_copy(
            src_ref=src, dst_ref=dst, send_sem=s, recv_sem=r, device_id=to, device_id_type=MESH)

    w_in = pltpu.make_async_copy(win_hbm, win, w_sem.at[0])
    w_dn = pltpu.make_async_copy(wdn_hbm, wdn, w_sem.at[1])
    w_in.start()
    w_dn.start()

    barrier = pltpu.get_barrier_semaphore()

    @pl.loop(1, RING)
    def _(d):
        pl.semaphore_signal(barrier, inc=1, device_id=in_ring(d)[1], device_id_type=MESH)

    pl.semaphore_signal(barrier, inc=1, device_id=mate, device_id_type=MESH)

    @pl.loop(1, PLANE)
    def _(d):
        pl.semaphore_signal(barrier, inc=1, device_id=in_plane(d)[1], device_id_type=MESH)

    routes = rt[...]
    erow = lax.broadcasted_iota(jnp.int32, (128, 128), 0)
    lane = lax.broadcasted_iota(jnp.int32, (128, 128), 1)
    named = erow == routes[0:1, :]
    for k in range(1, TOP):
        named = named | (erow == routes[k:k + 1, :])
    earlier = (erow < lax.rem(lane, TOK)).astype(jnp.bfloat16)
    count = jnp.dot(named.astype(jnp.bfloat16), earlier, preferred_element_type=jnp.float32)
    meta[zlo, 8:16, :] = wt[...]
    meta[zlo, 0:8, :] = jnp.full((8, 128), -16.0, jnp.float32)
    for k in range(TOP):
        chosen = routes[k:k + 1, :]
        slot = jnp.sum(jnp.where(erow == chosen, count, 0.0), axis=0, keepdims=True)
        meta[zlo, k:k + 1, :] = chosen.astype(jnp.float32) * 16.0 + slot
    tok_all[z] = tok[...]

    pl.semaphore_wait(barrier, RING - 1 + 1 + PLANE - 1)

    def run_copy(d):
        other = lax.rem(zlo + d, RUN)
        return other, remote(meta.at[zlo], meta.at[zlo], meta_s.at[d], meta_r.at[zlo],
                             (other * PLANE + here, tp))

    @pl.loop(1, RUN)
    def _(d):
        run_copy(d)[1].start()

    @pl.loop(1, RING)
    def _(d):
        remote(tok, tok_all.at[z], tok_s.at[d], tok_r.at[z], in_ring(d)[1]).start()

    @pl.loop(1, RUN)
    def _(d):
        other, copy = run_copy(d)
        remote(meta.at[other], meta.at[other], meta_s.at[d], meta_r.at[other],
               (other * PLANE + here, tp)).wait_recv()
        copy.wait_send()

    low = lax.broadcasted_iota(jnp.int32, (8, 128), 1) < TOK
    base = -16.0 * PLANE * zlo.astype(jnp.float32)
    row = lax.broadcasted_iota(jnp.int32, (ROWS, 128), 0).astype(jnp.float32)
    picks = []
    for pair in range(2):
        a, b = 2 * pair, 2 * pair + 1
        keys = jnp.where(low, meta[a, 0:8, :] + 4.0 * a, meta[b, 0:8, :] + 4.0 * b) + base
        weights = jnp.where(low, meta[a, 8:16, :], meta[b, 8:16, :])
        pick = jnp.zeros((ROWS, 128), jnp.float32)
        scaled = jnp.zeros((ROWS, 128), jnp.float32)
        for k in range(TOP):
            hit = row == keys[k:k + 1, :]
            pick = jnp.where(hit, 1.0, pick)
            scaled = jnp.where(hit, weights[k:k + 1, :], scaled)
        picks.append(pick.astype(jnp.bfloat16))
        hi = scaled.astype(jnp.bfloat16)
        cw_hi[:, pair * 128:(pair + 1) * 128] = hi
        cw_lo[:, pair * 128:(pair + 1) * 128] = (scaled - hi.astype(jnp.float32)).astype(jnp.bfloat16)
    pick = jnp.concatenate(picks, axis=1)

    @pl.loop(1, RING)
    def _(d):
        other, to = in_ring(d)
        remote(tok_all.at[other], tok_all.at[other], tok_s.at[d], tok_r.at[other], to).wait_recv()

    for half in range(2):
        rows = tok_all[half * RUN:(half + 1) * RUN].reshape(RUN * TOK, GRP)
        x = jnp.dot(pick, rows, preferred_element_type=jnp.float32).astype(jnp.bfloat16)
        xsend[:, :, half * GRP:(half + 1) * GRP] = x.reshape(PLANE, RUN * CAP, GRP)

    @pl.loop(1, PLANE)
    def _(d):
        other, to = in_plane(d)
        remote(xsend.at[other], xrecv.at[here], x_s.at[d], x_r.at[here], to).start()

    xrecv[here] = xsend[here]
    remote(xsend.at[here], xoth.at[here], o_s.at[here], o_r.at[here], mate).start()

    @pl.loop(1, PLANE)
    def _(d):
        other, to = in_plane(PLANE - d)
        remote(xrecv.at[other], xrecv.at[other], x_s.at[d], x_r.at[other], to).wait_recv()
        remote(xrecv.at[other], xoth.at[other], o_s.at[other], o_r.at[other], mate).start()

    @pl.loop(0, PLANE)
    def _(i):
        remote(xoth.at[i], xoth.at[i], o_s.at[i], o_r.at[i], mate).wait_recv()

    w_in.wait()
    w_dn.wait()

    nsrc = MBLK // (RUN * CAP)

    def times_in(x, which, group):
        col = pl.ds(pl.multiple_of(group * GRP, GRP), GRP)
        return lax.dot_general(x, win[which, :, col], (((1,), (1,)), ((), ())),
                               preferred_element_type=jnp.float32)

    def part_copy(m):
        at = pl.ds(pl.multiple_of(m * MBLK, MBLK), MBLK)
        return remote(psend.at[at], precv.at[at], p_s.at[m], p_r.at[m], mate)

    @pl.loop(0, ROWS // MBLK)
    def _(m):
        src = pl.ds(m * nsrc, nsrc)
        at = pl.ds(pl.multiple_of(m * MBLK, MBLK), MBLK)
        own = xrecv[src].reshape(MBLK, HALF)
        oth = xoth[src].reshape(MBLK, HALF)
        sums = []
        for which in range(2):
            total = times_in(own[:, :GRP], which, core) + times_in(own[:, GRP:], which, 2 + core)
            total += times_in(oth[:, :GRP], which, 1 - core) + times_in(oth[:, GRP:], which, 3 - core)
            sums.append(total)
        gate, up = sums
        hidden = (gate / (1.0 + jnp.exp(-gate)) * up).astype(jnp.bfloat16)
        for half in range(2):
            col = pl.ds(pl.multiple_of((half * 2 + 1 - core) * GRP, GRP), GRP)
            part = jnp.dot(hidden, wdn[:, col], preferred_element_type=jnp.float32)
            psend[at, half * GRP:(half + 1) * GRP] = part.astype(jnp.bfloat16)
        part_copy(m).start()
        for half in range(2):
            col = pl.ds(pl.multiple_of((half * 2 + core) * GRP, GRP), GRP)
            pown[at, half * GRP:(half + 1) * GRP] = jnp.dot(
                hidden, wdn[:, col], preferred_element_type=jnp.float32)

    @pl.loop(0, ROWS // MBLK)
    def _(m):
        at = pl.ds(pl.multiple_of(m * MBLK, MBLK), MBLK)
        part_copy(m).wait()
        total = pown[at, :] + precv[at, :].astype(jnp.float32)
        sbuf[pl.ds(m * nsrc, nsrc)] = total.astype(jnp.bfloat16).reshape(nsrc, RUN * CAP, HALF)

    @pl.loop(1, PLANE)
    def _(d):
        other, to = in_plane(d)
        remote(sbuf.at[other], back.at[here], b_s.at[d], b_r.at[here], to).start()

    back[here] = sbuf[here]

    @pl.loop(1, PLANE)
    def _(d):
        other, to = in_plane(PLANE - d)
        remote(back.at[other], back.at[other], b_s.at[d], b_r.at[other], to).wait_recv()

    contract = (((0,), (0,)), ((), ()))
    for half in range(2):
        rows = back[:, :, half * GRP:(half + 1) * GRP].reshape(ROWS, GRP)
        mixed = lax.dot_general(cw_hi[...], rows, contract, preferred_element_type=jnp.float32)
        mixed += lax.dot_general(cw_lo[...], rows, contract, preferred_element_type=jnp.float32)
        rsend[half * RUN:(half + 1) * RUN] = mixed.astype(jnp.bfloat16).reshape(RUN, TOK, GRP)

    @pl.loop(1, RING)
    def _(d):
        other, to = in_ring(d)
        remote(rsend.at[other], rrecv.at[z], q_s.at[d], q_r.at[z], to).start()

    rrecv[z] = rsend[z]

    @pl.loop(1, RING)
    def _(d):
        other, to = in_ring(d)
        remote(rrecv.at[other], rrecv.at[other], q_s.at[d], q_r.at[other], to).wait_recv()

    total = rrecv[0].astype(jnp.float32)
    for i in range(1, RING):
        total += rrecv[i].astype(jnp.float32)
    out[...] = total.astype(jnp.bfloat16)

    @pl.loop(1, RING)
    def _(d):
        other, to = in_ring(d)
        remote(tok, tok_all.at[z], tok_s.at[d], tok_r.at[z], to).wait_send()
        remote(rsend.at[other], rrecv.at[z], q_s.at[d], q_r.at[z], to).wait_send()

    @pl.loop(1, PLANE)
    def _(d):
        other, to = in_plane(d)
        remote(xsend.at[other], xrecv.at[here], x_s.at[d], x_r.at[here], to).wait_send()
        remote(sbuf.at[other], back.at[here], b_s.at[d], b_r.at[here], to).wait_send()

    @pl.loop(0, PLANE)
    def _(i):
        remote(xrecv.at[i], xoth.at[i], o_s.at[i], o_r.at[i], mate).wait_send()


def per_device(tokens, expert_in, expert_down, routes, route_weight):
    rt = jnp.pad(jnp.tile(routes.T, (1, 2)), ((0, 2), (0, 0)), constant_values=-1)
    wt = jnp.pad(jnp.tile(route_weight.T, (1, 2)), ((0, 2), (0, 0)))
    vmem = pl.BlockSpec(memory_space=pltpu.VMEM)
    hbm = pl.BlockSpec(memory_space=pl.ANY)
    bf16, f32 = jnp.bfloat16, jnp.float32
    chunk = (PLANE, RUN * CAP, HALF)
    dma = pltpu.SemaphoreType.DMA
    scratch = [
        pltpu.VMEM((2, FFG, 4 * GRP), bf16),
        pltpu.VMEM((FFG, 4 * GRP), bf16),
        pltpu.VMEM((RING, TOK, GRP), bf16),
        pltpu.VMEM((RUN, 16, 128), f32),
        pltpu.VMEM(chunk, bf16),
        pltpu.VMEM(chunk, bf16),
        pltpu.VMEM(chunk, bf16),
        pltpu.VMEM((ROWS, HALF), bf16),
        pltpu.VMEM((ROWS, HALF), bf16),
        pltpu.VMEM((ROWS, HALF), f32),
        pltpu.VMEM(chunk, bf16),
        pltpu.VMEM(chunk, bf16),
        pltpu.VMEM((ROWS, RUN * TOK), bf16),
        pltpu.VMEM((ROWS, RUN * TOK), bf16),
        pltpu.VMEM((RING, TOK, GRP), bf16),
        pltpu.VMEM((RING, TOK, GRP), bf16),
        dma((2,)),
        dma((RING,)), dma((RING,)), dma((RUN,)), dma((RUN,)),
        dma((PLANE,)), dma((PLANE,)), dma((PLANE,)), dma((PLANE,)),
        dma((ROWS // MBLK,)), dma((ROWS // MBLK,)),
        dma((PLANE,)), dma((PLANE,)),
        dma((RING,)), dma((RING,)),
    ]
    return pl.pallas_call(
        kernel,
        out_shape=jax.ShapeDtypeStruct((TOK, GRP), bf16),
        in_specs=[vmem, vmem, vmem, hbm, hbm],
        out_specs=vmem,
        scratch_shapes=scratch,
        compiler_params=pltpu.CompilerParams(
            collective_id=0, has_side_effects=True, vmem_limit_bytes=60 * 1024 * 1024),
        name="routed_experts",
    )(tokens, rt, wt, jnp.swapaxes(expert_in[0], 1, 2), expert_down.reshape(FFG, 4 * GRP))


def solution(mesh):
    placed = (
        P("req", "tp"),
        P("req", None, None, "tp"),
        P("req", "tp", None),
        P("req", None),
        P("req", None),
    )
    return jax.shard_map(
        per_device, mesh=mesh, in_specs=placed, out_specs=P("req", "tp"), check_vma=False
    )
```

```python
import jax
import jax.numpy as jnp
from jax import lax
from jax.experimental import pallas as pl
from jax.experimental.pallas import tpu as pltpu
from jax.sharding import PartitionSpec as P

MESH = pl.DeviceIdType.MESH
TOK, TOP, CAP = 64, 6, 4
PLANE, RUN, RING = 32, 4, 8
ROWS = PLANE * RUN * CAP
GRP, FFG = 512, 352
NEAR, FAR = 0, 1
STEPS = 4
MBLK = ROWS // STEPS


def kernel(tok, rt, wt, win_hbm, wdn_hbm, out,
           win, wdn, tok_all, meta, xsend, xrecv, xoth, psend, precv, pown, sbuf, back,
           cw_hi, cw_lo, rsend, rrecv,
           w_sem, tok_s, tok_r, meta_s, meta_r, x_s, x_r, o_s, o_r, p_s, p_r, b_s, b_r,
           q_s, q_r):
    req, tp = lax.axis_index("req"), lax.axis_index("tp")
    zlo, here = lax.div(req, PLANE), lax.rem(req, PLANE)
    y, x = lax.div(here, 4), lax.rem(here, 4)
    zhi, core = lax.div(tp, 2), lax.rem(tp, 2)
    z = zhi * RUN + zlo
    side = (zhi, 1 - zhi)

    def in_plane(other):
        return (zlo * PLANE + other, tp)

    def in_ring(other):
        return (lax.rem(other, RUN) * PLANE + here, lax.div(other, RUN) * 2 + core)

    def near_z(d):
        return zhi * RUN + lax.rem(zlo + d, RUN)

    def far_z(d):
        return (1 - zhi) * RUN + lax.rem(zlo + d, RUN)

    mate = (req, zhi * 2 + 1 - core)

    def remote(src, dst, s, r, to):
        return pltpu.make_async_remote_copy(
            src_ref=src, dst_ref=dst, send_sem=s, recv_sem=r, device_id=to, device_id_type=MESH)

    w_in = pltpu.make_async_copy(win_hbm, win, w_sem.at[0])
    w_dn = pltpu.make_async_copy(wdn_hbm, wdn, w_sem.at[1])
    w_in.start()
    w_dn.start()

    barrier = pltpu.get_barrier_semaphore()

    @pl.loop(1, RING)
    def _(d):
        pl.semaphore_signal(barrier, inc=1, device_id=in_ring(lax.rem(z + d, RING)),
                            device_id_type=MESH)

    pl.semaphore_signal(barrier, inc=1, device_id=mate, device_id_type=MESH)

    @pl.loop(1, PLANE)
    def _(d):
        pl.semaphore_signal(barrier, inc=1, device_id=in_plane(lax.rem(here + d, PLANE)),
                            device_id_type=MESH)

    routes = jnp.concatenate([rt[...], rt[...]], axis=1)
    erow = lax.broadcasted_iota(jnp.int32, (128, 128), 0)
    lane = lax.broadcasted_iota(jnp.int32, (128, 128), 1)
    named = erow == routes[0:1, :]
    for k in range(1, TOP):
        named = named | (erow == routes[k:k + 1, :])
    earlier = (erow < lax.rem(lane, TOK)).astype(jnp.bfloat16)
    count = jnp.dot(named.astype(jnp.bfloat16), earlier, preferred_element_type=jnp.float32)
    meta[zlo] = jnp.full((16, 128), -16.0, jnp.float32)
    meta[zlo, 8:8 + TOP, :] = jnp.concatenate([wt[...], wt[...]], axis=1)
    for k in range(TOP):
        chosen = routes[k:k + 1, :]
        slot = jnp.sum(jnp.where(erow == chosen, count, 0.0), axis=0, keepdims=True)
        meta[zlo, k:k + 1, :] = chosen.astype(jnp.float32) * 16.0 + slot
    tok_all[z] = tok[...]

    pl.semaphore_wait(barrier, RING - 1 + 1 + PLANE - 1)

    def meta_to(d):
        return remote(meta.at[zlo], meta.at[zlo], meta_s.at[d], meta_r.at[zlo],
                      in_ring(near_z(d)))

    def tok_to(other):
        return remote(tok, tok_all.at[z], tok_s.at[other], tok_r.at[z], in_ring(other))

    def tok_from(other):
        return remote(tok, tok_all.at[other], tok_s.at[other], tok_r.at[other], in_ring(other))

    @pl.loop(1, RUN)
    def _(d):
        meta_to(d).start()

    @pl.loop(1, RUN)
    def _(d):
        tok_to(near_z(d)).start()

    @pl.loop(1, RUN)
    def _(d):
        other = lax.rem(zlo + d, RUN)
        remote(meta.at[other], meta.at[other], meta_s.at[d], meta_r.at[other],
               in_ring(near_z(d))).wait_recv()

    low = lax.broadcasted_iota(jnp.int32, (8, 128), 1) < TOK
    base = -16.0 * PLANE * zlo.astype(jnp.float32)
    row = lax.broadcasted_iota(jnp.int32, (ROWS, 128), 0).astype(jnp.float32)

    def keys_of(pair):
        a, b = 2 * pair, 2 * pair + 1
        return jnp.where(low, meta[a, 0:8, :] + 4.0 * a, meta[b, 0:8, :] + 4.0 * b) + base

    picks = []
    for pair in range(2):
        keys = keys_of(pair)
        hit = row == keys[0:1, :]
        for k in range(1, TOP):
            hit = hit | (row == keys[k:k + 1, :])
        picks.append(hit.astype(jnp.bfloat16))
    pick = jnp.concatenate(picks, axis=1)

    def fill(half):
        rows = tok_all[pl.ds(side[half] * RUN, RUN)].reshape(RUN * TOK, GRP)
        got = jnp.dot(pick, rows, preferred_element_type=jnp.float32).astype(jnp.bfloat16)
        xsend[half] = got.reshape(PLANE, RUN * CAP, GRP)

    def block(m, which):
        off = lax.rem(8 - m, 8) if which == 0 else m + 1
        return off

    def send_rows(half):
        @pl.loop(1, PLANE)
        def _(i):
            m, r = lax.div(i, 8), lax.rem(i, 8)
            off = jnp.where(r < 4, lax.rem(8 - m, 8), m + 1)
            other = lax.rem(y + 8 - off, 8) * 4 + lax.rem(x + r, 4)
            remote(xsend.at[half, other], xrecv.at[half, here], x_s.at[half, other],
                   x_r.at[half, here], in_plane(other)).start()
        xrecv[half, here] = xsend[half, here]

    @pl.loop(1, RUN)
    def _(d):
        tok_from(near_z(d)).wait_recv()

    @pl.loop(0, RUN)
    def _(d):
        tok_to(far_z(d)).start()

    fill(NEAR)
    send_rows(NEAR)

    for pair in range(2):
        keys = keys_of(pair)
        weights = jnp.where(low, meta[2 * pair, 8:16, :], meta[2 * pair + 1, 8:16, :])
        scaled = jnp.zeros((ROWS, 128), jnp.float32)
        for k in range(TOP):
            scaled = jnp.where(row == keys[k:k + 1, :], weights[k:k + 1, :], scaled)
        hi = scaled.astype(jnp.bfloat16)
        cw_hi[:, pair * 128:(pair + 1) * 128] = hi
        cw_lo[:, pair * 128:(pair + 1) * 128] = (scaled - hi.astype(jnp.float32)).astype(jnp.bfloat16)

    @pl.loop(0, RUN)
    def _(d):
        tok_from(far_z(d)).wait_recv()

    fill(FAR)
    send_rows(FAR)

    def pass_on(half, line):
        at = pl.ds(line * 4, 4)
        return remote(xrecv.at[half, at], xoth.at[half, at], o_s.at[half, line],
                      o_r.at[half, line], mate)

    def arrive(half, off):
        line = lax.rem(y + off, 8)

        @pl.loop(0, 4)
        def _(i):
            other = line * 4 + i

            @pl.when(other != here)
            def _():
                remote(xrecv.at[half, other], xrecv.at[half, other], x_s.at[half, other],
                       x_r.at[half, other], in_plane(other)).wait_recv()
        pass_on(half, line).start()

    @pl.loop(0, STEPS)
    def _(m):
        for which in range(2):
            arrive(NEAR, block(m, which))

    w_in.wait()
    w_dn.wait()

    def times_in(lhs, which, group):
        col = pl.ds(pl.multiple_of(group * GRP, GRP), GRP)
        return lax.dot_general(lhs, win[which, :, col], (((1,), (1,)), ((), ())),
                               preferred_element_type=jnp.float32)

    def times_down(hidden, group):
        col = pl.ds(pl.multiple_of(group * GRP, GRP), GRP)
        return jnp.dot(hidden, wdn[:, col], preferred_element_type=jnp.float32)

    def part_copy(m):
        return remote(psend.at[m], precv.at[m], p_s.at[m], p_r.at[m], mate)

    def lines_of(m):
        return [lax.rem(y + block(m, which), 8) for which in range(2)]

    def send_back(half, line):
        @pl.loop(0, 4)
        def _(i):
            other = line * 4 + lax.rem(x + i, 4)

            @pl.when(other != here)
            def _():
                remote(sbuf.at[half, other], back.at[half, here], b_s.at[half, other],
                       b_r.at[half, here], in_plane(other)).start()

    def finish(m):
        part_copy(m).wait_recv()
        for half in (FAR, NEAR):
            total = pown[m, half] + precv[m, half].astype(jnp.float32)
            total = total.astype(jnp.bfloat16).reshape(2, 4, RUN * CAP, GRP)
            for which, line in enumerate(lines_of(m)):
                sbuf[half, pl.ds(line * 4, 4)] = total[which]
        for line in lines_of(m):
            send_back(FAR, line)

    @pl.loop(0, STEPS)
    def _(m):
        for which in range(2):
            arrive(FAR, block(m, which))

        @pl.when(m > 0)
        def _():
            finish(m - 1)

        lines = lines_of(m)
        for line in lines:
            for half in range(2):
                pass_on(half, line).wait_recv()
        parts = []
        for buf, of in ((xrecv, core), (xoth, 1 - core)):
            for half in range(2):
                lhs = jnp.concatenate(
                    [buf[half, pl.ds(line * 4, 4)].reshape(MBLK // 2, GRP) for line in lines], axis=0)
                parts.append((lhs, side[half] * 2 + of))
        gate = sum(times_in(lhs, 0, group) for lhs, group in parts)
        up = sum(times_in(lhs, 1, group) for lhs, group in parts)
        hidden = (gate / (1.0 + jnp.exp(-gate)) * up).astype(jnp.bfloat16)
        for half in range(2):
            psend[m, half] = times_down(hidden, side[half] * 2 + 1 - core).astype(jnp.bfloat16)
        part_copy(m).start()
        for half in range(2):
            pown[m, half] = times_down(hidden, side[half] * 2 + core)

    finish(STEPS - 1)

    @pl.loop(0, STEPS)
    def _(m):
        for line in lines_of(m):
            send_back(NEAR, line)

    contract = (((0,), (0,)), ((), ()))

    def ring_copy(dest):
        return remote(rsend.at[dest], rrecv.at[z], q_s.at[dest], q_r.at[z], in_ring(dest))

    def mix(half):
        back[half, here] = sbuf[half, here]

        @pl.loop(1, PLANE)
        def _(d):
            other = lax.rem(here + d, PLANE)
            remote(back.at[half, other], back.at[half, other], b_s.at[half, other],
                   b_r.at[half, other], in_plane(other)).wait_recv()
        rows = back[half].reshape(ROWS, GRP)
        mixed = lax.dot_general(cw_hi[...], rows, contract, preferred_element_type=jnp.float32)
        mixed += lax.dot_general(cw_lo[...], rows, contract, preferred_element_type=jnp.float32)
        rsend[pl.ds(side[half] * RUN, RUN)] = mixed.astype(jnp.bfloat16).reshape(RUN, TOK, GRP)

    mix(FAR)

    @pl.loop(0, RUN)
    def _(d):
        ring_copy(far_z(d)).start()

    mix(NEAR)

    @pl.loop(1, RUN)
    def _(d):
        ring_copy(near_z(d)).start()

    rrecv[z] = rsend[z]

    @pl.loop(1, PLANE)
    def _(d):
        other = lax.rem(here + d, PLANE)
        for half in range(2):
            remote(xsend.at[half, other], xrecv.at[half, here], x_s.at[half, other],
                   x_r.at[half, here], in_plane(other)).wait_send()
            remote(sbuf.at[half, other], back.at[half, here], b_s.at[half, other],
                   b_r.at[half, here], in_plane(other)).wait_send()

    @pl.loop(0, 8)
    def _(line):
        for half in range(2):
            pass_on(half, line).wait_send()

    @pl.loop(0, STEPS)
    def _(m):
        part_copy(m).wait_send()

    @pl.loop(1, RUN)
    def _(d):
        meta_to(d).wait_send()

    @pl.loop(1, RING)
    def _(d):
        tok_to(lax.rem(z + d, RING)).wait_send()

    @pl.loop(1, RING)
    def _(d):
        other = lax.rem(z + d, RING)
        remote(rrecv.at[other], rrecv.at[other], q_s.at[other], q_r.at[other],
               in_ring(other)).wait_recv()

    total = rrecv[0].astype(jnp.float32)
    for i in range(1, RING):
        total += rrecv[i].astype(jnp.float32)
    out[...] = total.astype(jnp.bfloat16)

    @pl.loop(1, RING)
    def _(d):
        ring_copy(lax.rem(z + d, RING)).wait_send()


def per_device(tokens, expert_in, expert_down, routes, route_weight):
    vmem = pl.BlockSpec(memory_space=pltpu.VMEM)
    hbm = pl.BlockSpec(memory_space=pl.ANY)
    bf16, f32 = jnp.bfloat16, jnp.float32
    chunks = (2, PLANE, RUN * CAP, GRP)
    part = (STEPS, 2, MBLK, GRP)
    dma = pltpu.SemaphoreType.DMA
    scratch = [
        pltpu.VMEM((2, FFG, 4 * GRP), bf16),
        pltpu.VMEM((FFG, 4 * GRP), bf16),
        pltpu.VMEM((RING, TOK, GRP), bf16),
        pltpu.VMEM((RUN, 16, 128), f32),
        pltpu.VMEM(chunks, bf16),
        pltpu.VMEM(chunks, bf16),
        pltpu.VMEM(chunks, bf16),
        pltpu.VMEM(part, bf16),
        pltpu.VMEM(part, bf16),
        pltpu.VMEM(part, f32),
        pltpu.VMEM(chunks, bf16),
        pltpu.VMEM(chunks, bf16),
        pltpu.VMEM((ROWS, RUN * TOK), bf16),
        pltpu.VMEM((ROWS, RUN * TOK), bf16),
        pltpu.VMEM((RING, TOK, GRP), bf16),
        pltpu.VMEM((RING, TOK, GRP), bf16),
        dma((2,)),
        dma((RING,)), dma((RING,)), dma((RUN,)), dma((RUN,)),
        dma((2, PLANE)), dma((2, PLANE)), dma((2, 8)), dma((2, 8)),
        dma((STEPS,)), dma((STEPS,)),
        dma((2, PLANE)), dma((2, PLANE)),
        dma((RING,)), dma((RING,)),
    ]
    return pl.pallas_call(
        kernel,
        out_shape=jax.ShapeDtypeStruct((TOK, GRP), bf16),
        in_specs=[vmem, vmem, vmem, hbm, hbm],
        out_specs=vmem,
        scratch_shapes=scratch,
        compiler_params=pltpu.CompilerParams(
            collective_id=0, has_side_effects=True, vmem_limit_bytes=60 * 1024 * 1024),
        name="routed_experts",
    )(tokens, routes.T, route_weight.T, jnp.swapaxes(expert_in[0], 1, 2),
      expert_down.reshape(FFG, 4 * GRP))


def solution(mesh):
    placed = (
        P("req", "tp"),
        P("req", None, None, "tp"),
        P("req", "tp", None),
        P("req", None),
        P("req", None),
    )
    return jax.shard_map(
        per_device, mesh=mesh, in_specs=placed, out_specs=P("req", "tp"), check_vma=False
    )
```

```python
import jax
import jax.numpy as jnp
from jax import lax
from jax.experimental import pallas as pl
from jax.experimental.pallas import tpu as pltpu
from jax.sharding import PartitionSpec as P

MESH = pl.DeviceIdType.MESH
TOK, TOP, CAP = 64, 6, 4
PLANE, RUN, RING = 32, 4, 8
ROWS = PLANE * RUN * CAP
GRP, FFG = 512, 352
NEAR, FAR = 0, 1
LINES = ((3, 5), (4, 0), (6, 2), (7, 1))
CROSS = (3, 5, 4)
STEPS = len(LINES)
MBLK = ROWS // STEPS


def kernel(tok, rt, wt, win_hbm, wdn_hbm, out,
           win, wdn, tok_all, meta, xsend, xrecv, xoth, psend, precv, pown, sbuf, back,
           cw_hi, cw_lo, rsend, rrecv,
           w_sem, tok_s, tok_r, meta_s, meta_r, x_s, x_r, o_s, o_r, p_s, p_r, b_s, b_r,
           q_s, q_r, zsend, zrecv, zx_s, zx_r, zb_s, zb_r):
    req, tp = lax.axis_index("req"), lax.axis_index("tp")
    zlo, here = lax.div(req, PLANE), lax.rem(req, PLANE)
    y, x = lax.div(here, 4), lax.rem(here, 4)
    zhi, core = lax.div(tp, 2), lax.rem(tp, 2)
    z = zhi * RUN + zlo
    side = (zhi, 1 - zhi)

    def in_plane(other):
        return (zlo * PLANE + other, tp)

    def in_ring(other):
        return (lax.rem(other, RUN) * PLANE + here, lax.div(other, RUN) * 2 + core)

    def near_z(d):
        return zhi * RUN + lax.rem(zlo + d, RUN)

    def far_z(d):
        return (1 - zhi) * RUN + lax.rem(zlo + d, RUN)

    mate = (req, zhi * 2 + 1 - core)
    opposite = (req, (1 - zhi) * 2 + core)

    def remote(src, dst, s, r, to):
        return pltpu.make_async_remote_copy(
            src_ref=src, dst_ref=dst, send_sem=s, recv_sem=r, device_id=to, device_id_type=MESH)

    w_in = pltpu.make_async_copy(win_hbm, win, w_sem.at[0])
    w_dn = pltpu.make_async_copy(wdn_hbm, wdn, w_sem.at[1])
    w_in.start()
    w_dn.start()

    barrier = pltpu.get_barrier_semaphore()

    @pl.loop(1, RING)
    def _(d):
        pl.semaphore_signal(barrier, inc=1, device_id=in_ring(lax.rem(z + d, RING)),
                            device_id_type=MESH)

    pl.semaphore_signal(barrier, inc=1, device_id=mate, device_id_type=MESH)

    @pl.loop(1, PLANE)
    def _(d):
        pl.semaphore_signal(barrier, inc=1, device_id=in_plane(lax.rem(here + d, PLANE)),
                            device_id_type=MESH)

    routes = jnp.concatenate([rt[...], rt[...]], axis=1)
    erow = lax.broadcasted_iota(jnp.int32, (128, 128), 0)
    lane = lax.broadcasted_iota(jnp.int32, (128, 128), 1)
    named = erow == routes[0:1, :]
    for k in range(1, TOP):
        named = named | (erow == routes[k:k + 1, :])
    earlier = (erow < lax.rem(lane, TOK)).astype(jnp.bfloat16)
    count = jnp.dot(named.astype(jnp.bfloat16), earlier, preferred_element_type=jnp.float32)
    meta[zlo] = jnp.full((16, 128), -16.0, jnp.float32)
    meta[zlo, 8:8 + TOP, :] = jnp.concatenate([wt[...], wt[...]], axis=1)
    for k in range(TOP):
        chosen = routes[k:k + 1, :]
        slot = jnp.sum(jnp.where(erow == chosen, count, 0.0), axis=0, keepdims=True)
        meta[zlo, k:k + 1, :] = chosen.astype(jnp.float32) * 16.0 + slot
    tok_all[z] = tok[...]

    pl.semaphore_wait(barrier, RING - 1 + 1 + PLANE - 1)

    def meta_to(d):
        return remote(meta.at[zlo], meta.at[zlo], meta_s.at[d], meta_r.at[zlo],
                      in_ring(near_z(d)))

    def tok_to(other):
        return remote(tok, tok_all.at[z], tok_s.at[other], tok_r.at[z], in_ring(other))

    def tok_from(other):
        return remote(tok, tok_all.at[other], tok_s.at[other], tok_r.at[other], in_ring(other))

    @pl.loop(1, RUN)
    def _(d):
        meta_to(d).start()

    @pl.loop(1, RUN)
    def _(d):
        tok_to(near_z(d)).start()

    @pl.loop(1, RUN)
    def _(d):
        other = lax.rem(zlo + d, RUN)
        remote(meta.at[other], meta.at[other], meta_s.at[d], meta_r.at[other],
               in_ring(near_z(d))).wait_recv()

    low = lax.broadcasted_iota(jnp.int32, (8, 128), 1) < TOK
    base = -16.0 * PLANE * zlo.astype(jnp.float32)
    row = lax.broadcasted_iota(jnp.int32, (ROWS, 128), 0).astype(jnp.float32)

    def keys_of(pair):
        a, b = 2 * pair, 2 * pair + 1
        return jnp.where(low, meta[a, 0:8, :] + 4.0 * a, meta[b, 0:8, :] + 4.0 * b) + base

    picks = []
    for pair in range(2):
        keys = keys_of(pair)
        hit = row == keys[0:1, :]
        for k in range(1, TOP):
            hit = hit | (row == keys[k:k + 1, :])
        picks.append(hit.astype(jnp.bfloat16))
    pick = jnp.concatenate(picks, axis=1)

    def fill(half):
        rows = tok_all[pl.ds(side[half] * RUN, RUN)].reshape(RUN * TOK, GRP)
        got = jnp.dot(pick, rows, preferred_element_type=jnp.float32).astype(jnp.bfloat16)
        xsend[half] = got.reshape(PLANE, RUN * CAP, GRP)

    def line_at(off):
        return lax.rem(y + off, 8)

    def crossing(half, off):
        return half == FAR and off in CROSS

    def send_rows(half):
        for off in sum(LINES, ()):
            if crossing(half, off):
                continue

            @pl.loop(1 if off == 0 else 0, 4)
            def _(i):
                other = line_at(8 - off) * 4 + lax.rem(x + i, 4)
                remote(xsend.at[half, other], xrecv.at[half, here], x_s.at[half, other],
                       x_r.at[half, here], in_plane(other)).start()
        xrecv[half, here] = xsend[half, here]

    @pl.loop(1, RUN)
    def _(d):
        tok_from(near_z(d)).wait_recv()

    @pl.loop(0, RUN)
    def _(d):
        tok_to(far_z(d)).start()

    fill(NEAR)
    send_rows(NEAR)

    for pair in range(2):
        keys = keys_of(pair)
        weights = jnp.where(low, meta[2 * pair, 8:16, :], meta[2 * pair + 1, 8:16, :])
        scaled = jnp.zeros((ROWS, 128), jnp.float32)
        for k in range(TOP):
            scaled = jnp.where(row == keys[k:k + 1, :], weights[k:k + 1, :], scaled)
        hi = scaled.astype(jnp.bfloat16)
        cw_hi[:, pair * 128:(pair + 1) * 128] = hi
        cw_lo[:, pair * 128:(pair + 1) * 128] = (scaled - hi.astype(jnp.float32)).astype(jnp.bfloat16)

    @pl.loop(0, RUN)
    def _(d):
        tok_from(far_z(d)).wait_recv()

    fill(FAR)
    send_rows(FAR)

    def pass_on(half, line):
        at = pl.ds(line * 4, 4)
        return remote(xrecv.at[half, at], xoth.at[half, at], o_s.at[half, line],
                      o_r.at[half, line], mate)

    def cross_rows(off):
        line = line_at(off)
        at = pl.ds(line * 4, 4)
        return remote(xrecv.at[NEAR, at], xrecv.at[FAR, at], zx_s.at[line], zx_r.at[line], opposite)

    def arrive(half, off):
        line = line_at(off)
        if crossing(half, off):
            cross_rows(off).wait_recv()
        else:
            @pl.loop(0, 4)
            def _(i):
                other = line * 4 + i

                @pl.when(other != here)
                def _():
                    remote(xrecv.at[half, other], xrecv.at[half, other], x_s.at[half, other],
                           x_r.at[half, other], in_plane(other)).wait_recv()
            if off in CROSS:
                cross_rows(off).start()
        pass_on(half, line).start()

    for off in sum(LINES, ()):
        arrive(NEAR, off)

    w_in.wait()
    w_dn.wait()

    def times_in(lhs, which, group):
        col = pl.ds(pl.multiple_of(group * GRP, GRP), GRP)
        return lax.dot_general(lhs, win[which, :, col], (((1,), (1,)), ((), ())),
                               preferred_element_type=jnp.float32)

    def times_down(hidden, group):
        col = pl.ds(pl.multiple_of(group * GRP, GRP), GRP)
        return jnp.dot(hidden, wdn[:, col], preferred_element_type=jnp.float32)

    def part_copy(m):
        return remote(psend.at[m], precv.at[m], p_s.at[m], p_r.at[m], mate)

    def send_back(half, off):
        @pl.loop(1 if off == 0 else 0, 4)
        def _(i):
            other = line_at(off) * 4 + lax.rem(x + i, 4)
            remote(sbuf.at[half, other], back.at[half, here], b_s.at[half, other],
                   b_r.at[half, here], in_plane(other)).start()

    def cross_back(off):
        k = CROSS.index(off)
        return remote(zsend.at[k], zrecv.at[k], zb_s.at[k], zb_r.at[k], opposite)

    def finish(m):
        part_copy(m).wait_recv()
        for half in (FAR, NEAR):
            total = pown[m, half] + precv[m, half].astype(jnp.float32)
            total = total.astype(jnp.bfloat16).reshape(2, 4, RUN * CAP, GRP)
            for which, off in enumerate(LINES[m]):
                if crossing(half, off):
                    zsend[CROSS.index(off)] = total[which]
                else:
                    sbuf[half, pl.ds(line_at(off) * 4, 4)] = total[which]
            if half == FAR:
                for off in LINES[m]:
                    if off in CROSS:
                        cross_back(off).start()
                    else:
                        send_back(FAR, off)

    def settle(m):
        for off in LINES[m]:
            if off in CROSS:
                cross_back(off).wait_recv()
                at = pl.ds(line_at(off) * 4, 4)
                total = sbuf[NEAR, at].astype(jnp.float32) + zrecv[CROSS.index(off)].astype(jnp.float32)
                sbuf[NEAR, at] = total.astype(jnp.bfloat16)
                send_back(NEAR, off)

    for off in CROSS:
        back[FAR, pl.ds(line_at(off) * 4, 4)] = jnp.zeros((4, RUN * CAP, GRP), jnp.bfloat16)

    for m in range(STEPS):
        for off in LINES[m]:
            arrive(FAR, off)
        if m >= 1:
            finish(m - 1)
        if m >= 2:
            settle(m - 2)
        lines = [line_at(off) for off in LINES[m]]
        for line in lines:
            for half in range(2):
                pass_on(half, line).wait_recv()
        parts = []
        for buf, of in ((xrecv, core), (xoth, 1 - core)):
            for half in range(2):
                lhs = jnp.concatenate(
                    [buf[half, pl.ds(line * 4, 4)].reshape(MBLK // 2, GRP) for line in lines], axis=0)
                parts.append((lhs, side[half] * 2 + of))
        gate = sum(times_in(lhs, 0, group) for lhs, group in parts)
        up = sum(times_in(lhs, 1, group) for lhs, group in parts)
        hidden = (gate / (1.0 + jnp.exp(-gate)) * up).astype(jnp.bfloat16)
        for half in range(2):
            psend[m, half] = times_down(hidden, side[half] * 2 + 1 - core).astype(jnp.bfloat16)
        part_copy(m).start()
        for half in range(2):
            pown[m, half] = times_down(hidden, side[half] * 2 + core)

    finish(STEPS - 1)
    for m in range(STEPS - 2, STEPS):
        settle(m)
    for off in sum(LINES, ()):
        if off not in CROSS:
            send_back(NEAR, off)

    contract = (((0,), (0,)), ((), ()))

    def ring_copy(dest):
        return remote(rsend.at[dest], rrecv.at[z], q_s.at[dest], q_r.at[z], in_ring(dest))

    def mix(half):
        back[half, here] = sbuf[half, here]

        for off in sum(LINES, ()):
            if crossing(half, off):
                continue

            @pl.loop(1 if off == 0 else 0, 4)
            def _(i):
                other = line_at(off) * 4 + lax.rem(x + i, 4)
                remote(back.at[half, other], back.at[half, other], b_s.at[half, other],
                       b_r.at[half, other], in_plane(other)).wait_recv()
        rows = back[half].reshape(ROWS, GRP)
        mixed = lax.dot_general(cw_hi[...], rows, contract, preferred_element_type=jnp.float32)
        mixed += lax.dot_general(cw_lo[...], rows, contract, preferred_element_type=jnp.float32)
        rsend[pl.ds(side[half] * RUN, RUN)] = mixed.astype(jnp.bfloat16).reshape(RUN, TOK, GRP)

    mix(FAR)

    @pl.loop(0, RUN)
    def _(d):
        ring_copy(far_z(d)).start()

    mix(NEAR)

    @pl.loop(1, RUN)
    def _(d):
        ring_copy(near_z(d)).start()

    rrecv[z] = rsend[z]

    for off in sum(LINES, ()):
        for half in range(2):
            if crossing(half, off):
                cross_rows(off).wait_send()
                cross_back(off).wait_send()
                continue

            @pl.loop(1 if off == 0 else 0, 4)
            def _(i):
                other = line_at(off) * 4 + lax.rem(x + i, 4)
                remote(xsend.at[half, other], xrecv.at[half, here], x_s.at[half, other],
                       x_r.at[half, here], in_plane(other)).wait_send()
                remote(sbuf.at[half, other], back.at[half, here], b_s.at[half, other],
                       b_r.at[half, here], in_plane(other)).wait_send()

    @pl.loop(0, 8)
    def _(line):
        for half in range(2):
            pass_on(half, line).wait_send()

    @pl.loop(0, STEPS)
    def _(m):
        part_copy(m).wait_send()

    @pl.loop(1, RUN)
    def _(d):
        meta_to(d).wait_send()

    @pl.loop(1, RING)
    def _(d):
        tok_to(lax.rem(z + d, RING)).wait_send()

    @pl.loop(1, RING)
    def _(d):
        other = lax.rem(z + d, RING)
        remote(rrecv.at[other], rrecv.at[other], q_s.at[other], q_r.at[other],
               in_ring(other)).wait_recv()

    total = rrecv[0].astype(jnp.float32)
    for i in range(1, RING):
        total += rrecv[i].astype(jnp.float32)
    out[...] = total.astype(jnp.bfloat16)

    @pl.loop(1, RING)
    def _(d):
        ring_copy(lax.rem(z + d, RING)).wait_send()


def per_device(tokens, expert_in, expert_down, routes, route_weight):
    vmem = pl.BlockSpec(memory_space=pltpu.VMEM)
    hbm = pl.BlockSpec(memory_space=pl.ANY)
    bf16, f32 = jnp.bfloat16, jnp.float32
    chunks = (2, PLANE, RUN * CAP, GRP)
    part = (STEPS, 2, MBLK, GRP)
    dma = pltpu.SemaphoreType.DMA
    scratch = [
        pltpu.VMEM((2, FFG, 4 * GRP), bf16),
        pltpu.VMEM((FFG, 4 * GRP), bf16),
        pltpu.VMEM((RING, TOK, GRP), bf16),
        pltpu.VMEM((RUN, 16, 128), f32),
        pltpu.VMEM(chunks, bf16),
        pltpu.VMEM(chunks, bf16),
        pltpu.VMEM(chunks, bf16),
        pltpu.VMEM(part, bf16),
        pltpu.VMEM(part, bf16),
        pltpu.VMEM(part, f32),
        pltpu.VMEM(chunks, bf16),
        pltpu.VMEM(chunks, bf16),
        pltpu.VMEM((ROWS, RUN * TOK), bf16),
        pltpu.VMEM((ROWS, RUN * TOK), bf16),
        pltpu.VMEM((RING, TOK, GRP), bf16),
        pltpu.VMEM((RING, TOK, GRP), bf16),
        dma((2,)),
        dma((RING,)), dma((RING,)), dma((RUN,)), dma((RUN,)),
        dma((2, PLANE)), dma((2, PLANE)), dma((2, 8)), dma((2, 8)),
        dma((STEPS,)), dma((STEPS,)),
        dma((2, PLANE)), dma((2, PLANE)),
        dma((RING,)), dma((RING,)),
        pltpu.VMEM((len(CROSS), 4, RUN * CAP, GRP), bf16),
        pltpu.VMEM((len(CROSS), 4, RUN * CAP, GRP), bf16),
        dma((8,)), dma((8,)), dma((len(CROSS),)), dma((len(CROSS),)),
    ]
    return pl.pallas_call(
        kernel,
        out_shape=jax.ShapeDtypeStruct((TOK, GRP), bf16),
        in_specs=[vmem, vmem, vmem, hbm, hbm],
        out_specs=vmem,
        scratch_shapes=scratch,
        compiler_params=pltpu.CompilerParams(
            collective_id=0, has_side_effects=True, vmem_limit_bytes=60 * 1024 * 1024),
        name="routed_experts",
    )(tokens, routes.T, route_weight.T, jnp.swapaxes(expert_in[0], 1, 2),
      expert_down.reshape(FFG, 4 * GRP))


def solution(mesh):
    placed = (
        P("req", "tp"),
        P("req", None, None, "tp"),
        P("req", "tp", None),
        P("req", None),
        P("req", None),
    )
    return jax.shard_map(
        per_device, mesh=mesh, in_specs=placed, out_specs=P("req", "tp"), check_vma=False
    )
```

```python
import jax
import jax.numpy as jnp
from jax import lax
from jax.experimental import pallas as pl
from jax.experimental.pallas import tpu as pltpu
from jax.sharding import PartitionSpec as P

MESH = pl.DeviceIdType.MESH
TOK, TOP, CAP = 64, 6, 4
PLANE, RUN, RING = 32, 4, 8
ROWS = PLANE * RUN * CAP
GRP, FFG = 512, 352
NEAR, FAR = 0, 1
LINES = ((4, 0), (3, 5), (6, 2), (7, 1))
CROSS = (4,)
STEPS = len(LINES)
MBLK = ROWS // STEPS


def kernel(tok, rt, wt, win_hbm, wdn_hbm, out,
           win, wdn, tok_all, meta, xsend, xrecv, xoth, psend, precv, pown, sbuf, back,
           cw_hi, cw_lo, rsend, rrecv,
           w_sem, tok_s, tok_r, meta_s, meta_r, x_s, x_r, o_s, o_r, p_s, p_r, b_s, b_r,
           q_s, q_r, zsend, zrecv, zx_s, zx_r, zb_s, zb_r):
    req, tp = lax.axis_index("req"), lax.axis_index("tp")
    zlo, here = lax.div(req, PLANE), lax.rem(req, PLANE)
    y, x = lax.div(here, 4), lax.rem(here, 4)
    zhi, core = lax.div(tp, 2), lax.rem(tp, 2)
    z = zhi * RUN + zlo
    side = (zhi, 1 - zhi)

    def in_plane(other):
        return (zlo * PLANE + other, tp)

    def in_ring(other):
        return (lax.rem(other, RUN) * PLANE + here, lax.div(other, RUN) * 2 + core)

    def near_z(d):
        return zhi * RUN + lax.rem(zlo + d, RUN)

    def far_z(d):
        return (1 - zhi) * RUN + lax.rem(zlo + d, RUN)

    mate = (req, zhi * 2 + 1 - core)
    opposite = (req, (1 - zhi) * 2 + core)

    def remote(src, dst, s, r, to):
        return pltpu.make_async_remote_copy(
            src_ref=src, dst_ref=dst, send_sem=s, recv_sem=r, device_id=to, device_id_type=MESH)

    w_in = pltpu.make_async_copy(win_hbm, win, w_sem.at[0])
    w_dn = pltpu.make_async_copy(wdn_hbm, wdn, w_sem.at[1])
    w_in.start()
    w_dn.start()

    barrier = pltpu.get_barrier_semaphore()

    @pl.loop(1, RING)
    def _(d):
        pl.semaphore_signal(barrier, inc=1, device_id=in_ring(lax.rem(z + d, RING)),
                            device_id_type=MESH)

    pl.semaphore_signal(barrier, inc=1, device_id=mate, device_id_type=MESH)

    @pl.loop(1, PLANE)
    def _(d):
        pl.semaphore_signal(barrier, inc=1, device_id=in_plane(lax.rem(here + d, PLANE)),
                            device_id_type=MESH)

    routes = jnp.concatenate([rt[...], rt[...]], axis=1)
    erow = lax.broadcasted_iota(jnp.int32, (128, 128), 0)
    lane = lax.broadcasted_iota(jnp.int32, (128, 128), 1)
    named = erow == routes[0:1, :]
    for k in range(1, TOP):
        named = named | (erow == routes[k:k + 1, :])
    earlier = (erow < lax.rem(lane, TOK)).astype(jnp.bfloat16)
    count = jnp.dot(named.astype(jnp.bfloat16), earlier, preferred_element_type=jnp.float32)
    meta[zlo] = jnp.full((16, 128), -16.0, jnp.float32)
    meta[zlo, 8:8 + TOP, :] = jnp.concatenate([wt[...], wt[...]], axis=1)
    for k in range(TOP):
        chosen = routes[k:k + 1, :]
        slot = jnp.sum(jnp.where(erow == chosen, count, 0.0), axis=0, keepdims=True)
        meta[zlo, k:k + 1, :] = chosen.astype(jnp.float32) * 16.0 + slot
    tok_all[z] = tok[...]

    pl.semaphore_wait(barrier, RING - 1 + 1 + PLANE - 1)

    def meta_to(d):
        return remote(meta.at[zlo], meta.at[zlo], meta_s.at[d], meta_r.at[zlo],
                      in_ring(near_z(d)))

    def tok_to(other):
        return remote(tok, tok_all.at[z], tok_s.at[other], tok_r.at[z], in_ring(other))

    def tok_from(other):
        return remote(tok, tok_all.at[other], tok_s.at[other], tok_r.at[other], in_ring(other))

    @pl.loop(1, RUN)
    def _(d):
        meta_to(d).start()

    @pl.loop(1, RUN)
    def _(d):
        tok_to(near_z(d)).start()

    @pl.loop(1, RUN)
    def _(d):
        other = lax.rem(zlo + d, RUN)
        remote(meta.at[other], meta.at[other], meta_s.at[d], meta_r.at[other],
               in_ring(near_z(d))).wait_recv()

    low = lax.broadcasted_iota(jnp.int32, (8, 128), 1) < TOK
    base = -16.0 * PLANE * zlo.astype(jnp.float32)
    row = lax.broadcasted_iota(jnp.int32, (ROWS, 128), 0).astype(jnp.float32)

    def keys_of(pair):
        a, b = 2 * pair, 2 * pair + 1
        return jnp.where(low, meta[a, 0:8, :] + 4.0 * a, meta[b, 0:8, :] + 4.0 * b) + base

    picks = []
    for pair in range(2):
        keys = keys_of(pair)
        hit = row == keys[0:1, :]
        for k in range(1, TOP):
            hit = hit | (row == keys[k:k + 1, :])
        picks.append(hit.astype(jnp.bfloat16))
    pick = jnp.concatenate(picks, axis=1)

    def fill(half):
        rows = tok_all[pl.ds(side[half] * RUN, RUN)].reshape(RUN * TOK, GRP)
        got = jnp.dot(pick, rows, preferred_element_type=jnp.float32).astype(jnp.bfloat16)
        xsend[half] = got.reshape(PLANE, RUN * CAP, GRP)

    def line_at(off):
        return lax.rem(y + off, 8)

    def crossing(half, off):
        return half == FAR and off in CROSS

    def send_rows(half):
        for off in sum(LINES, ()):
            if crossing(half, off):
                continue

            @pl.loop(1 if off == 0 else 0, 4)
            def _(i):
                other = line_at(8 - off) * 4 + lax.rem(x + i, 4)
                remote(xsend.at[half, other], xrecv.at[half, here], x_s.at[half, other],
                       x_r.at[half, here], in_plane(other)).start()
        xrecv[half, here] = xsend[half, here]

    @pl.loop(1, RUN)
    def _(d):
        tok_from(near_z(d)).wait_recv()

    @pl.loop(0, RUN)
    def _(d):
        tok_to(far_z(d)).start()

    fill(NEAR)
    send_rows(NEAR)

    for pair in range(2):
        keys = keys_of(pair)
        weights = jnp.where(low, meta[2 * pair, 8:16, :], meta[2 * pair + 1, 8:16, :])
        scaled = jnp.zeros((ROWS, 128), jnp.float32)
        for k in range(TOP):
            scaled = jnp.where(row == keys[k:k + 1, :], weights[k:k + 1, :], scaled)
        hi = scaled.astype(jnp.bfloat16)
        cw_hi[:, pair * 128:(pair + 1) * 128] = hi
        cw_lo[:, pair * 128:(pair + 1) * 128] = (scaled - hi.astype(jnp.float32)).astype(jnp.bfloat16)

    @pl.loop(0, RUN)
    def _(d):
        tok_from(far_z(d)).wait_recv()

    fill(FAR)
    send_rows(FAR)

    def pass_on(half, line):
        at = pl.ds(line * 4, 4)
        return remote(xrecv.at[half, at], xoth.at[half, at], o_s.at[half, line],
                      o_r.at[half, line], mate)

    def cross_rows(off):
        line = line_at(off)
        at = pl.ds(line * 4, 4)
        return remote(xrecv.at[NEAR, at], xrecv.at[FAR, at], zx_s.at[line], zx_r.at[line], opposite)

    def arrive(half, off):
        line = line_at(off)
        if crossing(half, off):
            cross_rows(off).wait_recv()
        else:
            @pl.loop(0, 4)
            def _(i):
                other = line * 4 + i

                @pl.when(other != here)
                def _():
                    remote(xrecv.at[half, other], xrecv.at[half, other], x_s.at[half, other],
                           x_r.at[half, other], in_plane(other)).wait_recv()
            if off in CROSS:
                cross_rows(off).start()
        pass_on(half, line).start()

    for off in sum(LINES, ()):
        arrive(NEAR, off)

    w_in.wait()
    w_dn.wait()

    def times_in(lhs, which, group):
        col = pl.ds(pl.multiple_of(group * GRP, GRP), GRP)
        return lax.dot_general(lhs, win[which, :, col], (((1,), (1,)), ((), ())),
                               preferred_element_type=jnp.float32)

    def times_down(hidden, group):
        col = pl.ds(pl.multiple_of(group * GRP, GRP), GRP)
        return jnp.dot(hidden, wdn[:, col], preferred_element_type=jnp.float32)

    def part_copy(m):
        return remote(psend.at[m], precv.at[m], p_s.at[m], p_r.at[m], mate)

    def send_back(half, off):
        @pl.loop(1 if off == 0 else 0, 4)
        def _(i):
            other = line_at(off) * 4 + lax.rem(x + i, 4)
            remote(sbuf.at[half, other], back.at[half, here], b_s.at[half, other],
                   b_r.at[half, here], in_plane(other)).start()

    def cross_back(off):
        k = CROSS.index(off)
        return remote(zsend.at[k], zrecv.at[k], zb_s.at[k], zb_r.at[k], opposite)

    def finish(m):
        part_copy(m).wait_recv()
        for half in (FAR, NEAR):
            total = pown[m, half] + precv[m, half].astype(jnp.float32)
            total = total.astype(jnp.bfloat16).reshape(2, 4, RUN * CAP, GRP)
            for which, off in enumerate(LINES[m]):
                if crossing(half, off):
                    zsend[CROSS.index(off)] = total[which]
                else:
                    sbuf[half, pl.ds(line_at(off) * 4, 4)] = total[which]
            if half == FAR:
                for off in LINES[m]:
                    if off in CROSS:
                        cross_back(off).start()
                    else:
                        send_back(FAR, off)

    def settle(m):
        for off in LINES[m]:
            if off in CROSS:
                cross_back(off).wait_recv()
                at = pl.ds(line_at(off) * 4, 4)
                total = sbuf[NEAR, at].astype(jnp.float32) + zrecv[CROSS.index(off)].astype(jnp.float32)
                sbuf[NEAR, at] = total.astype(jnp.bfloat16)
                send_back(NEAR, off)

    for off in CROSS:
        back[FAR, pl.ds(line_at(off) * 4, 4)] = jnp.zeros((4, RUN * CAP, GRP), jnp.bfloat16)

    for m in range(STEPS):
        for off in LINES[m]:
            arrive(FAR, off)
        if m >= 1:
            finish(m - 1)
        if m >= 2:
            settle(m - 2)
        lines = [line_at(off) for off in LINES[m]]
        for line in lines:
            for half in range(2):
                pass_on(half, line).wait_recv()
        parts = []
        for buf, of in ((xrecv, core), (xoth, 1 - core)):
            for half in range(2):
                lhs = jnp.concatenate(
                    [buf[half, pl.ds(line * 4, 4)].reshape(MBLK // 2, GRP) for line in lines], axis=0)
                parts.append((lhs, side[half] * 2 + of))
        gate = sum(times_in(lhs, 0, group) for lhs, group in parts)
        up = sum(times_in(lhs, 1, group) for lhs, group in parts)
        hidden = (gate / (1.0 + jnp.exp(-gate)) * up).astype(jnp.bfloat16)
        for half in range(2):
            psend[m, half] = times_down(hidden, side[half] * 2 + 1 - core).astype(jnp.bfloat16)
        part_copy(m).start()
        for half in range(2):
            pown[m, half] = times_down(hidden, side[half] * 2 + core)

    finish(STEPS - 1)
    for m in range(STEPS - 2, STEPS):
        settle(m)
    for off in sum(LINES, ()):
        if off not in CROSS:
            send_back(NEAR, off)

    contract = (((0,), (0,)), ((), ()))

    def ring_copy(dest):
        return remote(rsend.at[dest], rrecv.at[z], q_s.at[dest], q_r.at[z], in_ring(dest))

    def mix(half):
        back[half, here] = sbuf[half, here]

        for off in sum(LINES, ()):
            if crossing(half, off):
                continue

            @pl.loop(1 if off == 0 else 0, 4)
            def _(i):
                other = line_at(off) * 4 + lax.rem(x + i, 4)
                remote(back.at[half, other], back.at[half, other], b_s.at[half, other],
                       b_r.at[half, other], in_plane(other)).wait_recv()
        rows = back[half].reshape(ROWS, GRP)
        mixed = lax.dot_general(cw_hi[...], rows, contract, preferred_element_type=jnp.float32)
        mixed += lax.dot_general(cw_lo[...], rows, contract, preferred_element_type=jnp.float32)
        rsend[pl.ds(side[half] * RUN, RUN)] = mixed.astype(jnp.bfloat16).reshape(RUN, TOK, GRP)

    mix(FAR)

    @pl.loop(0, RUN)
    def _(d):
        ring_copy(far_z(d)).start()

    mix(NEAR)

    @pl.loop(1, RUN)
    def _(d):
        ring_copy(near_z(d)).start()

    rrecv[z] = rsend[z]

    for off in sum(LINES, ()):
        for half in range(2):
            if crossing(half, off):
                cross_rows(off).wait_send()
                cross_back(off).wait_send()
                continue

            @pl.loop(1 if off == 0 else 0, 4)
            def _(i):
                other = line_at(off) * 4 + lax.rem(x + i, 4)
                remote(xsend.at[half, other], xrecv.at[half, here], x_s.at[half, other],
                       x_r.at[half, here], in_plane(other)).wait_send()
                remote(sbuf.at[half, other], back.at[half, here], b_s.at[half, other],
                       b_r.at[half, here], in_plane(other)).wait_send()

    @pl.loop(0, 8)
    def _(line):
        for half in range(2):
            pass_on(half, line).wait_send()

    @pl.loop(0, STEPS)
    def _(m):
        part_copy(m).wait_send()

    @pl.loop(1, RUN)
    def _(d):
        meta_to(d).wait_send()

    @pl.loop(1, RING)
    def _(d):
        tok_to(lax.rem(z + d, RING)).wait_send()

    @pl.loop(1, RING)
    def _(d):
        other = lax.rem(z + d, RING)
        remote(rrecv.at[other], rrecv.at[other], q_s.at[other], q_r.at[other],
               in_ring(other)).wait_recv()

    total = rrecv[0].astype(jnp.float32)
    for i in range(1, RING):
        total += rrecv[i].astype(jnp.float32)
    out[...] = total.astype(jnp.bfloat16)

    @pl.loop(1, RING)
    def _(d):
        ring_copy(lax.rem(z + d, RING)).wait_send()


def per_device(tokens, expert_in, expert_down, routes, route_weight):
    vmem = pl.BlockSpec(memory_space=pltpu.VMEM)
    hbm = pl.BlockSpec(memory_space=pl.ANY)
    bf16, f32 = jnp.bfloat16, jnp.float32
    chunks = (2, PLANE, RUN * CAP, GRP)
    part = (STEPS, 2, MBLK, GRP)
    dma = pltpu.SemaphoreType.DMA
    scratch = [
        pltpu.VMEM((2, FFG, 4 * GRP), bf16),
        pltpu.VMEM((FFG, 4 * GRP), bf16),
        pltpu.VMEM((RING, TOK, GRP), bf16),
        pltpu.VMEM((RUN, 16, 128), f32),
        pltpu.VMEM(chunks, bf16),
        pltpu.VMEM(chunks, bf16),
        pltpu.VMEM(chunks, bf16),
        pltpu.VMEM(part, bf16),
        pltpu.VMEM(part, bf16),
        pltpu.VMEM(part, f32),
        pltpu.VMEM(chunks, bf16),
        pltpu.VMEM(chunks, bf16),
        pltpu.VMEM((ROWS, RUN * TOK), bf16),
        pltpu.VMEM((ROWS, RUN * TOK), bf16),
        pltpu.VMEM((RING, TOK, GRP), bf16),
        pltpu.VMEM((RING, TOK, GRP), bf16),
        dma((2,)),
        dma((RING,)), dma((RING,)), dma((RUN,)), dma((RUN,)),
        dma((2, PLANE)), dma((2, PLANE)), dma((2, 8)), dma((2, 8)),
        dma((STEPS,)), dma((STEPS,)),
        dma((2, PLANE)), dma((2, PLANE)),
        dma((RING,)), dma((RING,)),
        pltpu.VMEM((len(CROSS), 4, RUN * CAP, GRP), bf16),
        pltpu.VMEM((len(CROSS), 4, RUN * CAP, GRP), bf16),
        dma((8,)), dma((8,)), dma((len(CROSS),)), dma((len(CROSS),)),
    ]
    return pl.pallas_call(
        kernel,
        out_shape=jax.ShapeDtypeStruct((TOK, GRP), bf16),
        in_specs=[vmem, vmem, vmem, hbm, hbm],
        out_specs=vmem,
        scratch_shapes=scratch,
        compiler_params=pltpu.CompilerParams(
            collective_id=0, has_side_effects=True, vmem_limit_bytes=60 * 1024 * 1024),
        name="routed_experts",
    )(tokens, routes.T, route_weight.T, jnp.swapaxes(expert_in[0], 1, 2),
      expert_down.reshape(FFG, 4 * GRP))


def solution(mesh):
    placed = (
        P("req", "tp"),
        P("req", None, None, "tp"),
        P("req", "tp", None),
        P("req", None),
        P("req", None),
    )
    return jax.shard_map(
        per_device, mesh=mesh, in_specs=placed, out_specs=P("req", "tp"), check_vma=False
    )
```

```python
import jax
import jax.numpy as jnp
from jax import lax
from jax.experimental import pallas as pl
from jax.experimental.pallas import tpu as pltpu
from jax.sharding import PartitionSpec as P

MESH = pl.DeviceIdType.MESH
TOK, TOP, CAP = 64, 6, 4
PLANE, RUN, RING = 32, 4, 8
ROWS = PLANE * RUN * CAP
GRP, FFG = 512, 352
NEAR, FAR = 0, 1
LINES = ((4, 0), (3, 5), (6, 2), (7, 1))
CROSS = (4,)
STEPS = len(LINES)
MBLK = ROWS // STEPS


def kernel(tok, rt, wt, win_hbm, wdn_hbm, out,
           win, wdn, tok_all, meta, xsend, xrecv, xoth, psend, precv, pown, sbuf, back,
           cw_hi, cw_lo, rsend, rrecv,
           w_sem, tok_s, tok_r, meta_s, meta_r, x_s, x_r, o_s, o_r, p_s, p_r, b_s, b_r,
           q_s, q_r, zsend, zrecv, zx_s, zx_r, zb_s, zb_r):
    req, tp = lax.axis_index("req"), lax.axis_index("tp")
    zlo, here = lax.div(req, PLANE), lax.rem(req, PLANE)
    y, x = lax.div(here, 4), lax.rem(here, 4)
    zhi, core = lax.div(tp, 2), lax.rem(tp, 2)
    z = zhi * RUN + zlo
    side = (zhi, 1 - zhi)

    def in_plane(other):
        return (zlo * PLANE + other, tp)

    def in_ring(other):
        return (lax.rem(other, RUN) * PLANE + here, lax.div(other, RUN) * 2 + core)

    def near_z(d):
        return zhi * RUN + lax.rem(zlo + d, RUN)

    def far_z(d):
        return (1 - zhi) * RUN + lax.rem(zlo + d, RUN)

    mate = (req, zhi * 2 + 1 - core)
    opposite = (req, (1 - zhi) * 2 + core)

    def remote(src, dst, s, r, to):
        return pltpu.make_async_remote_copy(
            src_ref=src, dst_ref=dst, send_sem=s, recv_sem=r, device_id=to, device_id_type=MESH)

    w_in = pltpu.make_async_copy(win_hbm, win, w_sem.at[0])
    w_dn = pltpu.make_async_copy(wdn_hbm, wdn, w_sem.at[1])
    w_in.start()
    w_dn.start()

    barrier = pltpu.get_barrier_semaphore()

    @pl.loop(1, RING)
    def _(d):
        pl.semaphore_signal(barrier, inc=1, device_id=in_ring(lax.rem(z + d, RING)),
                            device_id_type=MESH)

    pl.semaphore_signal(barrier, inc=1, device_id=mate, device_id_type=MESH)

    @pl.loop(1, PLANE)
    def _(d):
        pl.semaphore_signal(barrier, inc=1, device_id=in_plane(lax.rem(here + d, PLANE)),
                            device_id_type=MESH)

    routes = jnp.concatenate([rt[...], rt[...]], axis=1)
    erow = lax.broadcasted_iota(jnp.int32, (128, 128), 0)
    lane = lax.broadcasted_iota(jnp.int32, (128, 128), 1)
    named = erow == routes[0:1, :]
    for k in range(1, TOP):
        named = named | (erow == routes[k:k + 1, :])
    earlier = (erow < lax.rem(lane, TOK)).astype(jnp.bfloat16)
    count = jnp.dot(named.astype(jnp.bfloat16), earlier, preferred_element_type=jnp.float32)
    meta[zlo] = jnp.full((16, 128), -16.0, jnp.float32)
    meta[zlo, 8:8 + TOP, :] = jnp.concatenate([wt[...], wt[...]], axis=1)
    for k in range(TOP):
        chosen = routes[k:k + 1, :]
        slot = jnp.sum(jnp.where(erow == chosen, count, 0.0), axis=0, keepdims=True)
        meta[zlo, k:k + 1, :] = chosen.astype(jnp.float32) * 16.0 + slot
    tok_all[z] = tok[...]

    pl.semaphore_wait(barrier, RING - 1 + 1 + PLANE - 1)

    def meta_to(d):
        return remote(meta.at[zlo], meta.at[zlo], meta_s.at[d], meta_r.at[zlo],
                      in_ring(near_z(d)))

    def tok_to(other):
        return remote(tok, tok_all.at[z], tok_s.at[other], tok_r.at[z], in_ring(other))

    def tok_from(other):
        return remote(tok, tok_all.at[other], tok_s.at[other], tok_r.at[other], in_ring(other))

    @pl.loop(1, RUN)
    def _(d):
        meta_to(d).start()

    @pl.loop(1, RUN)
    def _(d):
        tok_to(near_z(d)).start()

    @pl.loop(1, RUN)
    def _(d):
        other = lax.rem(zlo + d, RUN)
        remote(meta.at[other], meta.at[other], meta_s.at[d], meta_r.at[other],
               in_ring(near_z(d))).wait_recv()

    low = lax.broadcasted_iota(jnp.int32, (8, 128), 1) < TOK
    base = -16.0 * PLANE * zlo.astype(jnp.float32)
    row = lax.broadcasted_iota(jnp.int32, (ROWS, 128), 0).astype(jnp.float32)

    def keys_of(pair):
        a, b = 2 * pair, 2 * pair + 1
        return jnp.where(low, meta[a, 0:8, :] + 4.0 * a, meta[b, 0:8, :] + 4.0 * b) + base

    picks = []
    for pair in range(2):
        keys = keys_of(pair)
        hit = row == keys[0:1, :]
        for k in range(1, TOP):
            hit = hit | (row == keys[k:k + 1, :])
        picks.append(hit.astype(jnp.bfloat16))
    pick = jnp.concatenate(picks, axis=1)

    def fill(half):
        rows = tok_all[pl.ds(side[half] * RUN, RUN)].reshape(RUN * TOK, GRP)
        got = jnp.dot(pick, rows, preferred_element_type=jnp.float32).astype(jnp.bfloat16)
        xsend[half] = got.reshape(PLANE, RUN * CAP, GRP)

    def line_at(off):
        return lax.rem(y + off, 8)

    def crossing(half, off):
        return half == FAR and off in CROSS

    def send_rows(half):
        for off in sum(LINES, ()):
            if crossing(half, off):
                continue

            @pl.loop(1 if off == 0 else 0, 4)
            def _(i):
                other = line_at(8 - off) * 4 + lax.rem(x + i, 4)
                remote(xsend.at[half, other], xrecv.at[half, here], x_s.at[half, other],
                       x_r.at[half, here], in_plane(other)).start()
        xrecv[half, here] = xsend[half, here]

    @pl.loop(0, RUN)
    def _(d):
        tok_to(far_z(d)).start()

    @pl.loop(1, RUN)
    def _(d):
        tok_from(near_z(d)).wait_recv()

    fill(NEAR)
    send_rows(NEAR)

    for pair in range(2):
        keys = keys_of(pair)
        weights = jnp.where(low, meta[2 * pair, 8:16, :], meta[2 * pair + 1, 8:16, :])
        scaled = jnp.zeros((ROWS, 128), jnp.float32)
        for k in range(TOP):
            scaled = jnp.where(row == keys[k:k + 1, :], weights[k:k + 1, :], scaled)
        scaled = scaled.T
        hi = scaled.astype(jnp.bfloat16)
        cw_hi[pair * 128:(pair + 1) * 128, :] = hi
        cw_lo[pair * 128:(pair + 1) * 128, :] = (scaled - hi.astype(jnp.float32)).astype(jnp.bfloat16)

    @pl.loop(0, RUN)
    def _(d):
        tok_from(far_z(d)).wait_recv()

    fill(FAR)
    send_rows(FAR)

    def pass_on(half, line):
        at = pl.ds(line * 4, 4)
        return remote(xrecv.at[half, at], xoth.at[half, at], o_s.at[half, line],
                      o_r.at[half, line], mate)

    def cross_rows(off):
        line = line_at(off)
        at = pl.ds(line * 4, 4)
        return remote(xrecv.at[NEAR, at], xrecv.at[FAR, at], zx_s.at[line], zx_r.at[line], opposite)

    def arrive(half, off):
        line = line_at(off)
        if crossing(half, off):
            cross_rows(off).wait_recv()
        else:
            @pl.loop(0, 4)
            def _(i):
                other = line * 4 + i

                @pl.when(other != here)
                def _():
                    remote(xrecv.at[half, other], xrecv.at[half, other], x_s.at[half, other],
                           x_r.at[half, other], in_plane(other)).wait_recv()
            if off in CROSS:
                cross_rows(off).start()
        pass_on(half, line).start()

    for off in sum(LINES, ()):
        arrive(NEAR, off)

    w_in.wait()
    w_dn.wait()

    def times_in(lhs, which, group):
        col = pl.ds(pl.multiple_of(group * GRP, GRP), GRP)
        return lax.dot_general(lhs, win[which, :, col], (((1,), (1,)), ((), ())),
                               preferred_element_type=jnp.float32)

    def times_down(hidden, group):
        col = pl.ds(pl.multiple_of(group * GRP, GRP), GRP)
        return jnp.dot(hidden, wdn[:, col], preferred_element_type=jnp.float32)

    def part_copy(m):
        return remote(psend.at[m], precv.at[m], p_s.at[m], p_r.at[m], mate)

    def send_back(half, off):
        @pl.loop(1 if off == 0 else 0, 4)
        def _(i):
            other = line_at(off) * 4 + lax.rem(x + i, 4)
            remote(sbuf.at[half, other], back.at[half, here], b_s.at[half, other],
                   b_r.at[half, here], in_plane(other)).start()

    def cross_back(off):
        k = CROSS.index(off)
        return remote(zsend.at[k], zrecv.at[k], zb_s.at[k], zb_r.at[k], opposite)

    def finish(m):
        part_copy(m).wait_recv()
        for half in (FAR, NEAR):
            total = pown[m, half] + precv[m, half].astype(jnp.float32)
            total = total.astype(jnp.bfloat16).reshape(2, 4, RUN * CAP, GRP)
            for which, off in enumerate(LINES[m]):
                if crossing(half, off):
                    zsend[CROSS.index(off)] = total[which]
                else:
                    sbuf[half, pl.ds(line_at(off) * 4, 4)] = total[which]
            if half == FAR:
                for off in LINES[m]:
                    if off in CROSS:
                        cross_back(off).start()
                    else:
                        send_back(FAR, off)

    def settle(m):
        for off in LINES[m]:
            if off in CROSS:
                cross_back(off).wait_recv()
                at = pl.ds(line_at(off) * 4, 4)
                total = sbuf[NEAR, at].astype(jnp.float32) + zrecv[CROSS.index(off)].astype(jnp.float32)
                sbuf[NEAR, at] = total.astype(jnp.bfloat16)
                send_back(NEAR, off)

    for off in CROSS:
        back[FAR, pl.ds(line_at(off) * 4, 4)] = jnp.zeros((4, RUN * CAP, GRP), jnp.bfloat16)

    for m in range(STEPS):
        for off in LINES[m]:
            arrive(FAR, off)
        if m >= 1:
            finish(m - 1)
        if m >= 2:
            settle(m - 2)
        lines = [line_at(off) for off in LINES[m]]
        for line in lines:
            for half in range(2):
                pass_on(half, line).wait_recv()
        parts = []
        for buf, of in ((xrecv, core), (xoth, 1 - core)):
            for half in range(2):
                lhs = jnp.concatenate(
                    [buf[half, pl.ds(line * 4, 4)].reshape(MBLK // 2, GRP) for line in lines], axis=0)
                parts.append((lhs, side[half] * 2 + of))
        gate = sum(times_in(lhs, 0, group) for lhs, group in parts)
        up = sum(times_in(lhs, 1, group) for lhs, group in parts)
        hidden = (gate / (1.0 + jnp.exp(-gate)) * up).astype(jnp.bfloat16)
        for half in range(2):
            psend[m, half] = times_down(hidden, side[half] * 2 + 1 - core).astype(jnp.bfloat16)
        part_copy(m).start()
        for half in range(2):
            pown[m, half] = times_down(hidden, side[half] * 2 + core)

    finish(STEPS - 1)
    for m in range(STEPS - 2, STEPS):
        settle(m)
    for off in sum(LINES, ()):
        if off not in CROSS:
            send_back(NEAR, off)


    def ring_copy(dest):
        return remote(rsend.at[dest], rrecv.at[z], q_s.at[dest], q_r.at[z], in_ring(dest))

    def mix(half):
        back[half, here] = sbuf[half, here]

        for off in sum(LINES, ()):
            if crossing(half, off):
                continue

            @pl.loop(1 if off == 0 else 0, 4)
            def _(i):
                other = line_at(off) * 4 + lax.rem(x + i, 4)
                remote(back.at[half, other], back.at[half, other], b_s.at[half, other],
                       b_r.at[half, other], in_plane(other)).wait_recv()
        rows = back[half].reshape(ROWS, GRP)
        mixed = jnp.dot(cw_hi[...], rows, preferred_element_type=jnp.float32)
        mixed += jnp.dot(cw_lo[...], rows, preferred_element_type=jnp.float32)
        rsend[pl.ds(side[half] * RUN, RUN)] = mixed.astype(jnp.bfloat16).reshape(RUN, TOK, GRP)

    mix(FAR)

    @pl.loop(0, RUN)
    def _(d):
        ring_copy(far_z(d)).start()

    mix(NEAR)

    @pl.loop(1, RUN)
    def _(d):
        ring_copy(near_z(d)).start()

    rrecv[z] = rsend[z]

    for off in sum(LINES, ()):
        for half in range(2):
            if crossing(half, off):
                cross_rows(off).wait_send()
                cross_back(off).wait_send()
                continue

            @pl.loop(1 if off == 0 else 0, 4)
            def _(i):
                other = line_at(off) * 4 + lax.rem(x + i, 4)
                remote(xsend.at[half, other], xrecv.at[half, here], x_s.at[half, other],
                       x_r.at[half, here], in_plane(other)).wait_send()
                remote(sbuf.at[half, other], back.at[half, here], b_s.at[half, other],
                       b_r.at[half, here], in_plane(other)).wait_send()

    @pl.loop(0, 8)
    def _(line):
        for half in range(2):
            pass_on(half, line).wait_send()

    @pl.loop(0, STEPS)
    def _(m):
        part_copy(m).wait_send()

    @pl.loop(1, RUN)
    def _(d):
        meta_to(d).wait_send()

    @pl.loop(1, RING)
    def _(d):
        tok_to(lax.rem(z + d, RING)).wait_send()

    @pl.loop(1, RING)
    def _(d):
        other = lax.rem(z + d, RING)
        remote(rrecv.at[other], rrecv.at[other], q_s.at[other], q_r.at[other],
               in_ring(other)).wait_recv()

    total = rrecv[0].astype(jnp.float32)
    for i in range(1, RING):
        total += rrecv[i].astype(jnp.float32)
    out[...] = total.astype(jnp.bfloat16)

    @pl.loop(1, RING)
    def _(d):
        ring_copy(lax.rem(z + d, RING)).wait_send()


def per_device(tokens, expert_in, expert_down, routes, route_weight):
    vmem = pl.BlockSpec(memory_space=pltpu.VMEM)
    hbm = pl.BlockSpec(memory_space=pl.ANY)
    bf16, f32 = jnp.bfloat16, jnp.float32
    chunks = (2, PLANE, RUN * CAP, GRP)
    part = (STEPS, 2, MBLK, GRP)
    dma = pltpu.SemaphoreType.DMA
    scratch = [
        pltpu.VMEM((2, FFG, 4 * GRP), bf16),
        pltpu.VMEM((FFG, 4 * GRP), bf16),
        pltpu.VMEM((RING, TOK, GRP), bf16),
        pltpu.VMEM((RUN, 16, 128), f32),
        pltpu.VMEM(chunks, bf16),
        pltpu.VMEM(chunks, bf16),
        pltpu.VMEM(chunks, bf16),
        pltpu.VMEM(part, bf16),
        pltpu.VMEM(part, bf16),
        pltpu.VMEM(part, f32),
        pltpu.VMEM(chunks, bf16),
        pltpu.VMEM(chunks, bf16),
        pltpu.VMEM((RUN * TOK, ROWS), bf16),
        pltpu.VMEM((RUN * TOK, ROWS), bf16),
        pltpu.VMEM((RING, TOK, GRP), bf16),
        pltpu.VMEM((RING, TOK, GRP), bf16),
        dma((2,)),
        dma((RING,)), dma((RING,)), dma((RUN,)), dma((RUN,)),
        dma((2, PLANE)), dma((2, PLANE)), dma((2, 8)), dma((2, 8)),
        dma((STEPS,)), dma((STEPS,)),
        dma((2, PLANE)), dma((2, PLANE)),
        dma((RING,)), dma((RING,)),
        pltpu.VMEM((len(CROSS), 4, RUN * CAP, GRP), bf16),
        pltpu.VMEM((len(CROSS), 4, RUN * CAP, GRP), bf16),
        dma((8,)), dma((8,)), dma((len(CROSS),)), dma((len(CROSS),)),
    ]
    return pl.pallas_call(
        kernel,
        out_shape=jax.ShapeDtypeStruct((TOK, GRP), bf16),
        in_specs=[vmem, vmem, vmem, hbm, hbm],
        out_specs=vmem,
        scratch_shapes=scratch,
        compiler_params=pltpu.CompilerParams(
            collective_id=0, has_side_effects=True, vmem_limit_bytes=60 * 1024 * 1024),
        name="routed_experts",
    )(tokens, routes.T, route_weight.T, jnp.swapaxes(expert_in[0], 1, 2),
      expert_down.reshape(FFG, 4 * GRP))


def solution(mesh):
    placed = (
        P("req", "tp"),
        P("req", None, None, "tp"),
        P("req", "tp", None),
        P("req", None),
        P("req", None),
    )
    return jax.shard_map(
        per_device, mesh=mesh, in_specs=placed, out_specs=P("req", "tp"), check_vma=False
    )
```
